32 devices in a mesh: ra: 8 (over z, y), dec: 4 (over x, core).
Axes of the slice: x: 2, y: 2, z: 4, core: 2. Of those that a mesh axis runs over, the one named last changes fastest.
Arguments:
- start_block: float32 [64, 512, 128], P('ra', 'dec'), may hold values from -6 to 6
- edge_blocks: float32 [64, 4, 4, 132, 128], P('ra', 'dec'), may hold values from -0.25 to 0.25
- block_offsets: int32 [64, 4, 4], P('ra', 'dec'), may hold values from 0 to 4
- degree_counts: int32 [64, 512], P('ra', 'dec'), may hold values from 4 to 12
Outputs:
- basis: float32 [64, 512, 128], P('ra', 'dec')
- rfactor: float32 [128, 128], replicated
The draws below stay inside these ranges and needn't reach their ends.
All inputs are finite; a program needn't handle non-finite values.
Results may differ from the reference program's by a relative error of at most 0.0003.
Values sent between devices are 32-bit elements; how exact they have to be, the bound alone decides.
A program may use at most 64 MiB of HBM per device.

```python
import math
import jax
import jax.numpy as jnp
from jax import lax

CDEC = 128
COLS = 128
NBK = 4
NRA = 64
NDEC = 512
NODES = 32768
N_DEC = 4


def draw_start_block(key, part):
    key_common = jax.random.fold_in(key, 11)
    key_noise = jax.random.fold_in(key, 12)
    key_spread = jax.random.fold_in(key, 13)
    key_load = jax.random.fold_in(key, 16)
    key_load_signs = jax.random.fold_in(key, 17)
    spread = jnp.exp(jax.random.uniform(key_spread, (COLS,), jnp.float32, math.log(0.004), math.log(0.5)))
    load_signs = jnp.where(jax.random.bernoulli(key_load_signs, 0.5, (COLS,)), 1.0, -1.0).astype(jnp.float32)
    loadings = load_signs * jax.random.uniform(key_load, (COLS,), jnp.float32, 0.5, 1.5)
    common = jnp.clip(jax.random.normal(key_common, (NRA, NDEC, 1), jnp.float32), -2.5, 2.5)
    noise = jnp.clip(jax.random.normal(key_noise, (NRA, NDEC, COLS), jnp.float32), -3.0, 3.0)
    field = loadings * common + spread * noise
    return field.astype(jnp.float32)


def plant(values, own_key, least, high):
    dims = values.shape
    place = [jax.random.randint(jax.random.fold_in(own_key, axis), (), 0, dims[axis]) for axis in range(len(dims))]
    values = values.at[tuple(place)].set(least)
    longest = dims.index(max(dims))
    place[longest] = (place[longest] + 1) % dims[longest]
    return values.at[tuple(place)].set(high)


def block_levels(key, shape, pieces, smallest, largest):
    def one(dim, blocks):
        steps = jax.random.uniform(jax.random.fold_in(jax.random.fold_in(key, 6), dim), (blocks,), jnp.float32, smallest / len(pieces), largest / len(pieces))
        return jnp.repeat(jnp.exp(steps), shape[dim] // blocks).reshape((-1,) + (1,) * (len(shape) - dim - 1))

    gain = one(*pieces[0])
    for cut in pieces[1:]:
        gain = gain * one(*cut)
    return gain


def centred(rng, shape, scale, reach, shards=(), held_as=jnp.bfloat16):
    gain = block_levels(rng, shape, shards, -0.22, 0.18) if shards else 1.0
    entries = jax.random.normal(rng, shape, jnp.float32) * scale * gain
    return jnp.minimum(jnp.maximum(entries, -reach), reach).astype(held_as)


def setup_inputs(seed: int = 0) -> dict:
    arg_keys = jax.random.split(jax.random.key(seed), 5)
    return {
        "start_block": draw_start_block(jax.random.fold_in(arg_keys[4], 71), 0),
        "edge_blocks": centred(arg_keys[1], (NRA, N_DEC, NBK, CDEC + 4, CDEC), (NBK * (CDEC + 4)) ** -0.5, 0.25, ((0, 8), (1, 4)), jnp.float32),
        "block_offsets": plant(jax.random.randint(arg_keys[2], (NRA, N_DEC, NBK), 0, 5), jax.random.fold_in(arg_keys[2], 1), 0, 4).astype(jnp.int32),
        "degree_counts": plant(jax.random.randint(arg_keys[3], (NRA, NDEC), 4, 13), jax.random.fold_in(arg_keys[3], 1), 4, 12).astype(jnp.int32),
    }


def apply_operator(field, edge_blocks, block_offsets, degree_counts):
    padded = jnp.pad(field, ((0, 0), (2, 2), (0, 0)))
    starts = (jnp.arange(N_DEC) * CDEC).astype(jnp.int32)

    def window(part, begin):
        return lax.dynamic_slice_in_dim(part, begin, CDEC + 4, 1)

    def one_row(items):
        row_index, row_offsets, row_blocks, row_degree, row_field = items
        source = (row_index + row_offsets - 2) % NRA
        picked = padded[source]
        windows = jax.vmap(window)(picked, starts)
        coupled = jnp.einsum('dkqp,dkqc->dpc', row_blocks, windows, precision=lax.Precision.HIGHEST)
        coupled = coupled.reshape(NDEC, COLS)
        return row_degree.astype(field.dtype)[:, None] * row_field - coupled
    row_ids = jnp.arange(NRA).astype(jnp.int32)
    return lax.map(one_row, (row_ids, block_offsets, edge_blocks, degree_counts, field))

def cholesky_pass(matrix):
    gram = jnp.dot(matrix.T, matrix, precision=lax.Precision.HIGHEST)
    lower = jnp.linalg.cholesky(gram)
    identity = jnp.eye(COLS, dtype=matrix.dtype)
    inverse_lower = jax.scipy.linalg.solve_triangular(lower, identity, lower=True)
    ortho = jnp.dot(matrix, inverse_lower.T, precision=lax.Precision.HIGHEST)
    return (ortho, lower.T)

def reference(start_block, edge_blocks, block_offsets, degree_counts):
    previous = start_block
    image = apply_operator(start_block, edge_blocks, block_offsets, degree_counts)
    current = (image - 8.0 * start_block) / 4.0
    for order_index in range(3):
        image = apply_operator(current, edge_blocks, block_offsets, degree_counts)
        following = 2.0 * (image - 8.0 * current) / 4.0 - previous
        previous = current
        current = following
    filtered = current.reshape(NODES, COLS)
    ortho_first, upper_first = cholesky_pass(filtered)
    ortho_second, upper_second = cholesky_pass(ortho_first)
    scale = jnp.sqrt(jnp.asarray(NODES, dtype=filtered.dtype))
    basis = (ortho_second * scale).reshape(NRA, NDEC, COLS)
    rfactor = jnp.dot(upper_second, upper_first, precision=lax.Precision.HIGHEST) / scale
    return (basis, rfactor)
```

```python
import jax
import jax.numpy as jnp
from jax import lax
from jax.sharding import PartitionSpec as P


def padded(cells, sides, width, closed):
    for axis, dim in sides:
        count = lax.axis_size(axis)
        ends = count if closed else count - 1
        head = lax.slice_in_dim(cells, 0, width, axis=dim)
        tail = lax.slice_in_dim(cells, cells.shape[dim] - width, cells.shape[dim], axis=dim)
        cells = jnp.concatenate(
            [
                lax.ppermute(tail, axis, [(i, (i + 1) % count) for i in range(ends)]),
                cells,
                lax.ppermute(head, axis, [((i + 1) % count, i) for i in range(ends)]),
            ],
            axis=dim,
        )
    return cells


def extend_field(field):
    widened = padded(field, (("ra", 0),), 2, True)
    return padded(widened, (("dec", 1),), 2, False)


def apply_operator(field, local_blocks, local_offsets, degree_float):
    extended = extend_field(field)
    row_ids = lax.broadcasted_iota(jnp.int32, local_offsets.shape, 0)
    picked = extended[row_ids + local_offsets]
    coupled = jnp.einsum("ikqp,ikqc->ipc", local_blocks, picked, precision=lax.Precision.HIGHEST)
    return degree_float[:, :, None] * field - coupled


def lower_from_pairs(matrix):
    local_gram = jnp.dot(matrix.T, matrix, precision=lax.Precision.HIGHEST)
    return jnp.linalg.cholesky(lax.psum(local_gram, ("ra", "dec")))


def cholesky_pass(matrix):
    lower = lower_from_pairs(matrix)
    identity = jnp.eye(matrix.shape[1], dtype=matrix.dtype)
    inverse_lower = jax.scipy.linalg.solve_triangular(lower, identity, lower=True)
    ortho = jnp.dot(matrix, inverse_lower.T, precision=lax.Precision.HIGHEST)
    return (ortho, lower.T)


def on_device(start_block, edge_blocks, block_offsets, degree_counts):
    local_blocks = edge_blocks[:, 0]
    local_offsets = block_offsets[:, 0]
    degree_float = degree_counts.astype(jnp.float32)
    previous = start_block
    image = apply_operator(start_block, local_blocks, local_offsets, degree_float)
    current = (image - 8.0 * start_block) / 4.0
    for order_index in range(3):
        image = apply_operator(current, local_blocks, local_offsets, degree_float)
        following = 2.0 * (image - 8.0 * current) / 4.0 - previous
        previous = current
        current = following
    row_count, node_count, column_count = current.shape
    filtered = current.reshape(row_count * node_count, column_count)
    ortho_first, upper_first = cholesky_pass(filtered)
    ortho_second, upper_second = cholesky_pass(ortho_first)
    total_nodes = row_count * node_count * lax.axis_size("ra") * lax.axis_size("dec")
    scale = jnp.sqrt(jnp.asarray(total_nodes, dtype=jnp.float32))
    basis = (ortho_second * scale).reshape(row_count, node_count, column_count)
    rfactor = jnp.dot(upper_second, upper_first, precision=lax.Precision.HIGHEST) / scale
    return (basis, rfactor)


def solution(mesh):
    placed = (
        P("ra", "dec", None),
        P("ra", "dec", None, None, None),
        P("ra", "dec", None),
        P("ra", "dec"),
    )
    return jax.shard_map(
        on_device,
        mesh=mesh,
        in_specs=placed,
        out_specs=(P("ra", "dec", None), P()),
        check_vma=False,
    )
```

```python
import functools

import jax
import jax.numpy as jnp
from jax import lax
from jax.experimental import pallas as pl
from jax.experimental.pallas import tpu as pltpu
from jax.sharding import PartitionSpec as P

MESH = pl.DeviceIdType.MESH
F32 = jnp.float32
BF16 = jnp.bfloat16
STEPS = 4
HALO = 64


def three_parts(value):
    first = value.astype(BF16)
    rest = value - first.astype(F32)
    second = rest.astype(BF16)
    third = (rest - second.astype(F32)).astype(BF16)
    return first, second, third


def filter_kernel(
    ra_count, dec_count, offsets, start, edges, degrees, out,
    fields, low, high, left, right, wide, thin, wide_halo, thin_halo, edge_pair, edge_third, degree_cols,
    send_sem, recv_sem,
):
    rows = start.shape[0]
    ra = lax.axis_index("ra")
    dec = lax.axis_index("dec")
    up = lax.rem(ra + 1, ra_count)
    down = lax.rem(ra + ra_count - 1, ra_count)
    has_left = dec > 0
    has_right = dec < dec_count - 1

    barrier = pltpu.get_barrier_semaphore()

    def greet(r, d):
        pl.semaphore_signal(barrier, inc=1, device_id=(r, d), device_id_type=MESH)

    greet(up, dec)
    greet(down, dec)

    @pl.when(has_left)
    def _():
        for r in (up, down, ra):
            greet(r, dec - 1)

    @pl.when(has_right)
    def _():
        for r in (up, down, ra):
            greet(r, dec + 1)

    pl.semaphore_wait(barrier, 2 + 3 * jnp.where(has_left, 1, 0) + 3 * jnp.where(has_right, 1, 0))

    def copy(version, slot, source, target, r, d):
        return pltpu.make_async_remote_copy(
            src_ref=source, dst_ref=target, send_sem=send_sem.at[version, slot], recv_sem=recv_sem.at[version, slot],
            device_id=(r, d), device_id_type=MESH,
        )

    def copies(version):
        field = start if version == 0 else fields.at[version - 1]
        first, last = pl.ds(0, 2), pl.ds(rows - 2, 2)
        head, tail = pl.ds(0, 8), pl.ds(120, 8)
        top, bottom, middle = pl.ds(0, 2), pl.ds(rows + 2, 2), pl.ds(2, rows)
        to_right, to_left = left.at[version], right.at[version]
        ring = [
            copy(version, 0, field.at[last], low.at[version], up, dec),
            copy(version, 1, field.at[first], high.at[version], down, dec),
        ]
        rightward = [
            copy(version, 2, field.at[last, tail], to_right.at[top], up, dec + 1),
            copy(version, 3, field.at[first, tail], to_right.at[bottom], down, dec + 1),
            copy(version, 4, field.at[:, tail], to_right.at[middle], ra, dec + 1),
        ]
        leftward = [
            copy(version, 5, field.at[last, head], to_left.at[top], up, dec - 1),
            copy(version, 6, field.at[first, head], to_left.at[bottom], down, dec - 1),
            copy(version, 7, field.at[:, head], to_left.at[middle], ra, dec - 1),
        ]
        return ring, rightward, leftward

    def start_edges(version):
        ring, rightward, leftward = copies(version)
        for c in ring:
            c.start()

        @pl.when(has_right)
        def _():
            for c in rightward[:2]:
                c.start()

        @pl.when(has_left)
        def _():
            for c in leftward[:2]:
                c.start()

    def start_middle(version):
        _, rightward, leftward = copies(version)

        @pl.when(has_right)
        def _():
            rightward[2].start()

        @pl.when(has_left)
        def _():
            leftward[2].start()

    def receive(version):
        ring, rightward, leftward = copies(version)
        for c in ring:
            c.wait_recv()

        @pl.when(has_left)
        def _():
            for c in rightward:
                c.wait_recv()

        @pl.when(has_right)
        def _():
            for c in leftward:
                c.wait_recv()

    def finish_sends(version):
        ring, rightward, leftward = copies(version)
        for c in ring:
            c.wait_send()

        @pl.when(has_right)
        def _():
            for c in rightward:
                c.wait_send()

        @pl.when(has_left)
        def _():
            for c in leftward:
                c.wait_send()

    def put(turn, place, value):
        first, second, third = three_parts(value)
        wide[turn, place, :, 0:128] = first
        wide[turn, place, :, 128:256] = second
        thin[turn, place] = third

    start_edges(0)
    start_middle(0)

    for version in range(STEPS):
        @pl.when(dec == 0)
        def _():
            left[version] = jnp.zeros_like(left[version])

        @pl.when(dec == dec_count - 1)
        def _():
            right[version] = jnp.zeros_like(right[version])

    turned = jnp.transpose(degrees[...].astype(F32))
    for row in range(rows):
        degree_cols[row] = jnp.broadcast_to(turned[:, row : row + 1], (128, 128)) - 8.0

    def prepare(row, carry):
        put(0, row + 2, start[row])
        pieces = [edges[row, k, 2:130, :].T for k in range(4)]
        blank = jnp.zeros((6, 128), F32)
        tips = []
        for k in range(4):
            tips += [blank, edges[row, k, 0:2, :], edges[row, k, 130:132, :], blank]
        pieces.append(jnp.concatenate(tips, axis=0).T)
        turned_edges = jnp.concatenate(pieces, axis=1)
        first, second, third = three_parts(turned_edges)
        edge_pair[row, 0:128] = first
        edge_pair[row, 128:256] = second
        edge_third[row] = third
        return carry

    lax.fori_loop(0, rows, prepare, 0)

    def one_row(version, row):
        turn = version % 2
        places = [row + offsets[row, k] for k in range(4)]
        both = jnp.concatenate([wide[turn, p] for p in places] + [wide_halo[p] for p in places], axis=0)
        last = jnp.concatenate([thin[turn, p] for p in places] + [thin_halo[p] for p in places], axis=0)
        pair = edge_pair[row]
        square = jnp.dot(pair, both, preferred_element_type=F32)
        small = jnp.dot(pair[0:128], last, preferred_element_type=F32) + jnp.dot(
            edge_third[row], both[:, 0:128], preferred_element_type=F32
        )
        small = square[128:256, 128:256] + small
        coupled = square[0:128, 0:128] + ((square[0:128, 128:256] + square[128:256, 0:128]) + small)
        field = start[row] if version == 0 else fields[version - 1, row]
        image = degree_cols[row] * field - coupled
        if version == 0:
            return image * 0.25
        before = start[row] if version == 1 else fields[version - 2, row]
        return image * 0.5 - before

    def run_row(version, row):
        value = one_row(version, row)
        if version == STEPS - 1:
            out[row] = value
        else:
            fields[version, row] = value
            put((version + 1) % 2, row + 2, value)

    for version in range(STEPS):
        turn = version % 2
        receive(version)
        for i in range(2):
            put(turn, i, low[version, i])
            put(turn, rows + 2 + i, high[version, i])

        def halo(place, carry):
            tips = jnp.concatenate([left[version, place], right[version, place]], axis=0)
            first, second, third = three_parts(tips)
            wide_halo[place, :, 0:128] = first
            wide_halo[place, :, 128:256] = second
            thin_halo[place] = third
            return carry

        lax.fori_loop(0, rows + 4, halo, 0)

        def boundary(i, carry):
            run_row(version, i + (rows - 4) * (i // 2))
            return carry

        def interior(i, carry):
            run_row(version, i + 2)
            return carry

        lax.fori_loop(0, 4, boundary, 0)
        if version < STEPS - 1:
            start_edges(version + 1)
        lax.fori_loop(0, rows - 4, interior, 0)
        if version < STEPS - 1:
            start_middle(version + 1)

    for version in range(STEPS):
        finish_sends(version)


def filtered_field(start_block, edges, offsets, degrees):
    rows = start_block.shape[0]
    vmem = pl.BlockSpec(memory_space=pltpu.VMEM)
    depth = 4 * 128 + HALO
    return pl.pallas_call(
        functools.partial(filter_kernel, lax.axis_size("ra"), lax.axis_size("dec")),
        out_shape=jax.ShapeDtypeStruct(start_block.shape, F32),
        in_specs=[pl.BlockSpec(memory_space=pltpu.SMEM), vmem, vmem, vmem],
        out_specs=vmem,
        scratch_shapes=[
            pltpu.VMEM((STEPS - 1, rows, 128, 128), F32),
            pltpu.VMEM((STEPS, 2, 128, 128), F32),
            pltpu.VMEM((STEPS, 2, 128, 128), F32),
            pltpu.VMEM((STEPS, rows + 4, 8, 128), F32),
            pltpu.VMEM((STEPS, rows + 4, 8, 128), F32),
            pltpu.VMEM((2, rows + 4, 128, 256), BF16),
            pltpu.VMEM((2, rows + 4, 128, 128), BF16),
            pltpu.VMEM((rows + 4, 16, 256), BF16),
            pltpu.VMEM((rows + 4, 16, 128), BF16),
            pltpu.VMEM((rows, 256, depth), BF16),
            pltpu.VMEM((rows, 128, depth), BF16),
            pltpu.VMEM((rows, 128, 128), F32),
            pltpu.SemaphoreType.DMA((STEPS, 8)),
            pltpu.SemaphoreType.DMA((STEPS, 8)),
        ],
        compiler_params=pltpu.CompilerParams(collective_id=0, has_side_effects=True, vmem_limit_bytes=48 * 2**20),
        name="filter",
    )(offsets, start_block, edges, degrees)


def gram_kernel(ra_count, dec_count, matrix, total, sums, came, send_sem, recv_sem):
    ra = lax.axis_index("ra")
    dec = lax.axis_index("dec")
    partners = []
    for bit in range(dec_count.bit_length() - 1):
        step = 2**bit
        partners.append((ra, dec + step - 2 * step * lax.rem(dec // step, 2)))
    for bit in range(ra_count.bit_length() - 1):
        step = 2**bit
        partners.append((ra + step - 2 * step * lax.rem(ra // step, 2), dec))
    barrier = pltpu.get_barrier_semaphore()
    for partner in partners:
        pl.semaphore_signal(barrier, inc=1, device_id=partner, device_id_type=MESH)
    local = lax.dot_general(
        matrix[...], matrix[...], (((0,), (0,)), ((), ())), precision=lax.Precision.HIGHEST, preferred_element_type=F32
    )
    pl.semaphore_wait(barrier, len(partners))
    for level, partner in enumerate(partners):
        sums[level] = local
        move = pltpu.make_async_remote_copy(
            src_ref=sums.at[level], dst_ref=came.at[level], send_sem=send_sem.at[level], recv_sem=recv_sem.at[level],
            device_id=partner, device_id_type=MESH,
        )
        move.start()
        move.wait()
        local = local + came[level]
    total[...] = local


def whole_gram(matrix):
    vmem = pl.BlockSpec(memory_space=pltpu.VMEM)
    levels = lax.axis_size(("ra", "dec")).bit_length() - 1
    return pl.pallas_call(
        functools.partial(gram_kernel, lax.axis_size("ra"), lax.axis_size("dec")),
        out_shape=jax.ShapeDtypeStruct((128, 128), F32),
        in_specs=[vmem],
        out_specs=vmem,
        scratch_shapes=[
            pltpu.VMEM((levels, 128, 128), F32),
            pltpu.VMEM((levels, 128, 128), F32),
            pltpu.SemaphoreType.DMA((levels,)),
            pltpu.SemaphoreType.DMA((levels,)),
        ],
        compiler_params=pltpu.CompilerParams(collective_id=1, has_side_effects=True),
        name="gram",
    )(matrix)


def cholesky_pass(matrix):
    lower = jnp.linalg.cholesky(whole_gram(matrix))
    identity = jnp.eye(matrix.shape[1], dtype=matrix.dtype)
    inverse_lower = jax.scipy.linalg.solve_triangular(lower, identity, lower=True)
    ortho = jnp.dot(matrix, inverse_lower.T, precision=lax.Precision.HIGHEST)
    return (ortho, lower.T)


def on_device(start_block, edge_blocks, block_offsets, degree_counts):
    current = filtered_field(start_block, edge_blocks[:, 0], block_offsets[:, 0], degree_counts)
    row_count, node_count, column_count = current.shape
    filtered = current.reshape(row_count * node_count, column_count)
    ortho_first, upper_first = cholesky_pass(filtered)
    ortho_second, upper_second = cholesky_pass(ortho_first)
    total_nodes = row_count * node_count * lax.axis_size("ra") * lax.axis_size("dec")
    scale = jnp.sqrt(jnp.asarray(total_nodes, dtype=jnp.float32))
    basis = (ortho_second * scale).reshape(row_count, node_count, column_count)
    rfactor = jnp.dot(upper_second, upper_first, precision=lax.Precision.HIGHEST) / scale
    return (basis, rfactor)


def solution(mesh):
    placed = (
        P("ra", "dec", None),
        P("ra", "dec", None, None, None),
        P("ra", "dec", None),
        P("ra", "dec"),
    )
    return jax.shard_map(
        on_device,
        mesh=mesh,
        in_specs=placed,
        out_specs=(P("ra", "dec", None), P()),
        check_vma=False,
    )
```

```python
import functools

import jax
import jax.numpy as jnp
from jax import lax
from jax.experimental import pallas as pl
from jax.experimental.pallas import tpu as pltpu
from jax.sharding import PartitionSpec as P

MESH = pl.DeviceIdType.MESH
F32 = jnp.float32
BF16 = jnp.bfloat16
STEPS = 4
HALO = 64


def three_parts(value):
    first = value.astype(BF16)
    rest = value - first.astype(F32)
    second = rest.astype(BF16)
    third = (rest - second.astype(F32)).astype(BF16)
    return first, second, third


def filter_kernel(
    ra_count, dec_count, offsets, start, edges, degrees, out, local,
    fields, low, high, left, right, wide, thin, wide_halo, thin_halo, edge_pair, edge_third, degree_cols,
    send_sem, recv_sem,
):
    rows = start.shape[0]
    ra = lax.axis_index("ra")
    dec = lax.axis_index("dec")
    up = lax.rem(ra + 1, ra_count)
    down = lax.rem(ra + ra_count - 1, ra_count)
    has_left = dec > 0
    has_right = dec < dec_count - 1

    barrier = pltpu.get_barrier_semaphore()

    def greet(r, d):
        pl.semaphore_signal(barrier, inc=1, device_id=(r, d), device_id_type=MESH)

    greet(up, dec)
    greet(down, dec)

    @pl.when(has_left)
    def _():
        for r in (up, down, ra):
            greet(r, dec - 1)

    @pl.when(has_right)
    def _():
        for r in (up, down, ra):
            greet(r, dec + 1)

    pl.semaphore_wait(barrier, 2 + 3 * jnp.where(has_left, 1, 0) + 3 * jnp.where(has_right, 1, 0))

    def copy(version, slot, source, target, r, d):
        return pltpu.make_async_remote_copy(
            src_ref=source, dst_ref=target, send_sem=send_sem.at[version, slot], recv_sem=recv_sem.at[version, slot],
            device_id=(r, d), device_id_type=MESH,
        )

    def copies(version):
        field = start if version == 0 else fields.at[version - 1]
        first, last = pl.ds(0, 2), pl.ds(rows - 2, 2)
        head, tail = pl.ds(0, 8), pl.ds(120, 8)
        top, bottom, middle = pl.ds(0, 2), pl.ds(rows + 2, 2), pl.ds(2, rows)
        to_right, to_left = left.at[version], right.at[version]
        ring = [
            copy(version, 0, field.at[last], low.at[version], up, dec),
            copy(version, 1, field.at[first], high.at[version], down, dec),
        ]
        rightward = [
            copy(version, 2, field.at[last, tail], to_right.at[top], up, dec + 1),
            copy(version, 3, field.at[first, tail], to_right.at[bottom], down, dec + 1),
            copy(version, 4, field.at[:, tail], to_right.at[middle], ra, dec + 1),
        ]
        leftward = [
            copy(version, 5, field.at[last, head], to_left.at[top], up, dec - 1),
            copy(version, 6, field.at[first, head], to_left.at[bottom], down, dec - 1),
            copy(version, 7, field.at[:, head], to_left.at[middle], ra, dec - 1),
        ]
        return ring, rightward, leftward

    def start_edges(version):
        ring, rightward, leftward = copies(version)
        for c in ring:
            c.start()

        @pl.when(has_right)
        def _():
            for c in rightward[:2]:
                c.start()

        @pl.when(has_left)
        def _():
            for c in leftward[:2]:
                c.start()

    def start_middle(version):
        _, rightward, leftward = copies(version)

        @pl.when(has_right)
        def _():
            rightward[2].start()

        @pl.when(has_left)
        def _():
            leftward[2].start()

    def receive(version):
        ring, rightward, leftward = copies(version)
        for c in ring:
            c.wait_recv()

        @pl.when(has_left)
        def _():
            for c in rightward:
                c.wait_recv()

        @pl.when(has_right)
        def _():
            for c in leftward:
                c.wait_recv()

    def finish_sends(version):
        ring, rightward, leftward = copies(version)
        for c in ring:
            c.wait_send()

        @pl.when(has_right)
        def _():
            for c in rightward:
                c.wait_send()

        @pl.when(has_left)
        def _():
            for c in leftward:
                c.wait_send()

    def put(turn, place, value):
        first, second, third = three_parts(value)
        wide[turn, place, :, 0:128] = first
        wide[turn, place, :, 128:256] = second
        thin[turn, place] = third

    start_edges(0)
    start_middle(0)

    for version in range(STEPS):
        @pl.when(dec == 0)
        def _():
            left[version] = jnp.zeros_like(left[version])

        @pl.when(dec == dec_count - 1)
        def _():
            right[version] = jnp.zeros_like(right[version])

    turned = jnp.transpose(degrees[...].astype(F32))
    for row in range(rows):
        degree_cols[row] = jnp.broadcast_to(turned[:, row : row + 1], (128, 128)) - 8.0

    def prepare(row, carry):
        put(0, row + 2, start[row])
        pieces = [edges[row, k, 2:130, :].T for k in range(4)]
        blank = jnp.zeros((6, 128), F32)
        tips = []
        for k in range(4):
            tips += [blank, edges[row, k, 0:2, :], edges[row, k, 130:132, :], blank]
        pieces.append(jnp.concatenate(tips, axis=0).T)
        turned_edges = jnp.concatenate(pieces, axis=1)
        first, second, third = three_parts(turned_edges)
        edge_pair[row, 0:128] = first
        edge_pair[row, 128:256] = second
        edge_third[row] = third
        return carry

    lax.fori_loop(0, rows, prepare, 0)

    def one_row(version, row):
        turn = version % 2
        places = [row + offsets[row, k] for k in range(4)]
        both = jnp.concatenate([wide[turn, p] for p in places] + [wide_halo[p] for p in places], axis=0)
        last = jnp.concatenate([thin[turn, p] for p in places] + [thin_halo[p] for p in places], axis=0)
        pair = edge_pair[row]
        square = jnp.dot(pair, both, preferred_element_type=F32)
        small = jnp.dot(pair[0:128], last, preferred_element_type=F32) + jnp.dot(
            edge_third[row], both[:, 0:128], preferred_element_type=F32
        )
        small = square[128:256, 128:256] + small
        coupled = square[0:128, 0:128] + ((square[0:128, 128:256] + square[128:256, 0:128]) + small)
        field = start[row] if version == 0 else fields[version - 1, row]
        image = degree_cols[row] * field - coupled
        if version == 0:
            return image * 0.25
        before = start[row] if version == 1 else fields[version - 2, row]
        return image * 0.5 - before

    def run_row(version, row):
        value = one_row(version, row)
        if version == STEPS - 1:
            out[row] = value
        else:
            fields[version, row] = value
            put((version + 1) % 2, row + 2, value)

    for version in range(STEPS):
        turn = version % 2
        receive(version)
        for i in range(2):
            put(turn, i, low[version, i])
            put(turn, rows + 2 + i, high[version, i])

        def halo(place, carry):
            tips = jnp.concatenate([left[version, place], right[version, place]], axis=0)
            first, second, third = three_parts(tips)
            wide_halo[place, :, 0:128] = first
            wide_halo[place, :, 128:256] = second
            thin_halo[place] = third
            return carry

        lax.fori_loop(0, rows + 4, halo, 0)

        def boundary(i, carry):
            run_row(version, i + (rows - 4) * (i // 2))
            return carry

        def interior(i, carry):
            run_row(version, i + 2)
            return carry

        lax.fori_loop(0, 4, boundary, 0)
        if version < STEPS - 1:
            start_edges(version + 1)
        lax.fori_loop(0, rows - 4, interior, 0)
        if version < STEPS - 1:
            start_middle(version + 1)

    local[...] = own_gram(out[...].reshape(rows * 128, 128))
    for version in range(STEPS):
        finish_sends(version)


def filtered_field(start_block, edges, offsets, degrees):
    rows = start_block.shape[0]
    vmem = pl.BlockSpec(memory_space=pltpu.VMEM)
    depth = 4 * 128 + HALO
    return pl.pallas_call(
        functools.partial(filter_kernel, lax.axis_size("ra"), lax.axis_size("dec")),
        out_shape=(jax.ShapeDtypeStruct(start_block.shape, F32), jax.ShapeDtypeStruct((128, 128), F32)),
        in_specs=[pl.BlockSpec(memory_space=pltpu.SMEM), vmem, vmem, vmem],
        out_specs=(vmem, vmem),
        scratch_shapes=[
            pltpu.VMEM((STEPS - 1, rows, 128, 128), F32),
            pltpu.VMEM((STEPS, 2, 128, 128), F32),
            pltpu.VMEM((STEPS, 2, 128, 128), F32),
            pltpu.VMEM((STEPS, rows + 4, 8, 128), F32),
            pltpu.VMEM((STEPS, rows + 4, 8, 128), F32),
            pltpu.VMEM((2, rows + 4, 128, 256), BF16),
            pltpu.VMEM((2, rows + 4, 128, 128), BF16),
            pltpu.VMEM((rows + 4, 16, 256), BF16),
            pltpu.VMEM((rows + 4, 16, 128), BF16),
            pltpu.VMEM((rows, 256, depth), BF16),
            pltpu.VMEM((rows, 128, depth), BF16),
            pltpu.VMEM((rows, 128, 128), F32),
            pltpu.SemaphoreType.DMA((STEPS, 8)),
            pltpu.SemaphoreType.DMA((STEPS, 8)),
        ],
        compiler_params=pltpu.CompilerParams(collective_id=0, has_side_effects=True, vmem_limit_bytes=48 * 2**20),
        name="filter",
    )(offsets, start_block, edges, degrees)


def sum_kernel(ra_count, dec_count, local, total, sums, came, pair_came, send_sem, recv_sem, pair_send, pair_recv):
    ra = lax.axis_index("ra")
    dec = lax.axis_index("dec")
    side = lax.rem(dec, 2)
    mine = pl.ds(pl.multiple_of(side * 64, 64), 64)
    other = pl.ds(pl.multiple_of(64 - side * 64, 64), 64)
    pair = (ra, dec + 1 - 2 * side)
    partners = []
    for bit in range(1, dec_count.bit_length() - 1):
        step = 2**bit
        partners.append((ra, dec + step - 2 * step * lax.rem(dec // step, 2)))
    for bit in range(ra_count.bit_length() - 1):
        step = 2**bit
        partners.append((ra + step - 2 * step * lax.rem(ra // step, 2), dec))
    barrier = pltpu.get_barrier_semaphore()
    for partner in [pair] + partners:
        pl.semaphore_signal(barrier, inc=1, device_id=partner, device_id_type=MESH)
    pl.semaphore_wait(barrier, len(partners) + 1)
    gather = pltpu.make_async_remote_copy(
        src_ref=local.at[other], dst_ref=pair_came, send_sem=pair_send.at[0], recv_sem=pair_recv.at[0],
        device_id=pair, device_id_type=MESH,
    )
    gather.start()
    gather.wait()
    value = local[mine] + pair_came[...]
    for level, partner in enumerate(partners):
        sums[level] = value
        move = pltpu.make_async_remote_copy(
            src_ref=sums.at[level], dst_ref=came.at[level], send_sem=send_sem.at[level], recv_sem=recv_sem.at[level],
            device_id=partner, device_id_type=MESH,
        )
        move.start()
        move.wait()
        value = value + came[level]
    total[mine] = value
    share = pltpu.make_async_remote_copy(
        src_ref=total.at[mine], dst_ref=total.at[mine], send_sem=pair_send.at[1], recv_sem=pair_recv.at[1],
        device_id=pair, device_id_type=MESH,
    )
    share.start()
    share.wait()


def sum_over_devices(local):
    vmem = pl.BlockSpec(memory_space=pltpu.VMEM)
    levels = lax.axis_size(("ra", "dec")).bit_length() - 2
    return pl.pallas_call(
        functools.partial(sum_kernel, lax.axis_size("ra"), lax.axis_size("dec")),
        out_shape=jax.ShapeDtypeStruct((128, 128), F32),
        in_specs=[vmem],
        out_specs=vmem,
        scratch_shapes=[
            pltpu.VMEM((levels, 64, 128), F32),
            pltpu.VMEM((levels, 64, 128), F32),
            pltpu.VMEM((64, 128), F32),
            pltpu.SemaphoreType.DMA((levels,)),
            pltpu.SemaphoreType.DMA((levels,)),
            pltpu.SemaphoreType.DMA((2,)),
            pltpu.SemaphoreType.DMA((2,)),
        ],
        compiler_params=pltpu.CompilerParams(collective_id=1, has_side_effects=True),
        name="sum_gram",
    )(local)


def factor(gram):
    tile = (8, 128)
    sub = lax.broadcasted_iota(jnp.int32, tile, 0)
    lane = lax.broadcasted_iota(jnp.int32, tile, 1)
    blocks = 16
    gram = 0.5 * (gram + gram.T)
    body = [gram[8 * m : 8 * m + 8] for m in range(blocks)]
    side = [jnp.where(lane == sub + 8 * m, 1.0, 0.0).astype(F32) for m in range(blocks)]
    upper, inverse = [], []

    def row_of(value, i):
        return jnp.broadcast_to(value[i : i + 1], tile)

    for k in range(blocks):
        columns = {
            m: [jnp.broadcast_to(body[m][:, 8 * k + i : 8 * k + i + 1], tile) for i in range(8)] for m in range(k, blocks)
        }
        left, right = body[k], side[k]
        upper_rows, inverse_rows = left, right
        left_rows, right_rows = [], []
        for i in range(8):
            pivot = row_of(columns[k][i], i)
            root = lax.rsqrt(pivot)
            root = root * (1.5 - 0.5 * pivot * root * root)
            entries = [row_of(columns[k][j], i) * root for j in range(i + 1, 8)]
            for m in range(k, blocks):
                columns[m][i] = columns[m][i] * root
                for j in range(i + 1, 8):
                    columns[m][j] = columns[m][j] - columns[m][i] * entries[j - i - 1]
            left_row, right_row = row_of(left, i) * root, row_of(right, i) * root
            left_rows.append(left_row)
            right_rows.append(right_row)
            upper_rows = jnp.where(sub == i, left_row, upper_rows)
            inverse_rows = jnp.where(sub == i, right_row, inverse_rows)
            left = left - columns[k][i] * left_row
            right = right - columns[k][i] * right_row
        upper.append(jnp.where(lane >= sub + 8 * k, upper_rows, 0.0))
        inverse.append(jnp.where(lane <= sub + 8 * k, inverse_rows, 0.0))
        for m in range(k + 1, blocks):
            for i in range(8):
                body[m] = body[m] - columns[m][i] * left_rows[i]
                side[m] = side[m] - columns[m][i] * right_rows[i]
    return jnp.concatenate(upper, axis=0), jnp.concatenate(inverse, axis=0)


def own_gram(matrix):
    return lax.dot_general(
        matrix, matrix, (((0,), (0,)), ((), ())), precision=lax.Precision.HIGHEST, preferred_element_type=F32
    )


def times_transposed(matrix, inverse):
    return lax.dot_general(
        matrix, inverse, (((1,), (1,)), ((), ())), precision=lax.Precision.HIGHEST, preferred_element_type=F32
    )


def first_kernel(gram, matrix, ortho, upper, local):
    upper[...], inverse = factor(gram[...])
    value = times_transposed(matrix[...], inverse)
    ortho[...] = value
    local[...] = own_gram(value)


def second_kernel(scale, gram, matrix, upper_first, basis, rfactor):
    upper, inverse = factor(gram[...])
    basis[...] = times_transposed(matrix[...], inverse) * scale
    rfactor[...] = jnp.dot(upper, upper_first[...], precision=lax.Precision.HIGHEST, preferred_element_type=F32) / scale


def on_device(start_block, edge_blocks, block_offsets, degree_counts):
    current, local = filtered_field(start_block, edge_blocks[:, 0], block_offsets[:, 0], degree_counts)
    row_count, node_count, column_count = current.shape
    filtered = current.reshape(row_count * node_count, column_count)
    total_nodes = row_count * node_count * lax.axis_size("ra") * lax.axis_size("dec")
    scale = total_nodes**0.5
    vmem = pl.BlockSpec(memory_space=pltpu.VMEM)
    tall = jax.ShapeDtypeStruct(filtered.shape, F32)
    square = jax.ShapeDtypeStruct((128, 128), F32)
    ortho, upper_first, local = pl.pallas_call(
        first_kernel, out_shape=(tall, square, square), in_specs=[vmem] * 2, out_specs=(vmem,) * 3, name="first_pass"
    )(sum_over_devices(local), filtered)
    basis, rfactor = pl.pallas_call(
        functools.partial(second_kernel, scale), out_shape=(tall, square), in_specs=[vmem] * 3, out_specs=(vmem,) * 2,
        name="second_pass",
    )(sum_over_devices(local), ortho, upper_first)
    return (basis.reshape(current.shape), rfactor)


def solution(mesh):
    placed = (
        P("ra", "dec", None),
        P("ra", "dec", None, None, None),
        P("ra", "dec", None),
        P("ra", "dec"),
    )
    return jax.shard_map(
        on_device,
        mesh=mesh,
        in_specs=placed,
        out_specs=(P("ra", "dec", None), P()),
        check_vma=False,
    )
```
